32 devices in a mesh: tok: 8 (over z, x), tp: 4 (over y, core).
Axes of the slice: x: 2, y: 2, z: 4, core: 2. Of those that a mesh axis runs over, the one named last changes fastest.
Arguments:
- tokens: bfloat16 [36928, 768], P('tok'), may hold values from -6 to 6
- slot_index: int32 [36928], P('tok'), may hold values from -1 to 18477, as said below
- segment: int32 [36928], P('tok'), may hold values from 0 to 3, as said below
- router: float32 [768], replicated, may hold values from -0.21875 to 0.21875
- first_norm: float32 [2, 768], replicated, may hold values from -0.6 to 1.3
- qkv_weight: bfloat16 [768, 3, 768], P(None, None, 'tp'), may hold values from -0.21875 to 0.21875
- qv_bias: float32 [2, 768], P(None, 'tp'), may hold values from -4 to 4
- out_weight: bfloat16 [768, 768], P('tp'), may hold values from -1.75 to 1.75
- out_bias: float32 [768], P('tp'), may hold values from -4 to 4
- second_norm: float32 [2, 768], replicated, may hold values from -0.6 to 1.3
- up_weight: bfloat16 [768, 3072], P(None, 'tp'), may hold values from -0.21875 to 0.21875
- up_bias: float32 [3072], P('tp'), may hold values from -4 to 4
- down_weight: bfloat16 [3072, 768], P('tp'), may hold values from -0.109375 to 0.109375
- down_bias: float32 [768], P('tp'), may hold values from -4 to 4
- cotangent: bfloat16 [36928, 768], P('tok'), may hold values from -6 to 6
Outputs:
- layer_out: bfloat16 [36928, 768], P('tok', 'tp')
- d_tokens: float32 [36928, 768], P('tok', 'tp')
- d_qkv_weight: float32 [768, 3, 768], P(None, None, 'tp')
- d_qv_bias: float32 [2, 768], P(None, 'tp')
- d_out_weight: float32 [768, 768], P('tp')
- d_out_bias: float32 [768], P('tp')
- d_up_weight: float32 [768, 3072], P(None, 'tp')
- d_up_bias: float32 [3072], P('tp')
- d_down_weight: float32 [3072, 768], P('tp')
- d_down_bias: float32 [768], P('tp')
- d_first_norm: float32 [2, 768], P(None, 'tp')
- d_second_norm: float32 [2, 768], P(None, 'tp')
- d_router: float32 [768], P('tp')
The draws below stay inside these ranges and needn't reach their ends.
Inputs may be any that keep to these rules, and one draw needn't show every extreme that they name: `slot_index`: -1 where the router leaves a patch out; else a slot of the compact buffers, slot // 289 being its row buffer, owned by index slot // 2312 of tok. No slot is named twice, each buffer's named slots are its lowest ones, every index of tok holds exactly 2168 selected patches and owns 2168 named slots, and at most 271 of the selected patches of one index of tok lie in rows of one owner. `segment`: within a row buffer the segments of named slots never fall from one slot to the next.
All inputs are finite; a program needn't handle non-finite values.
Results may differ from the reference program's by a relative error of at most 0.013.
Values may be sent and summed in bfloat16 or wider, within the bound.
No kernel may reach another device: no remote copies, remote signals or barrier semaphores. Data moves between devices by JAX's collectives and lax.ppermute only.
A program may use at most 320 MiB of HBM per device.

```python
import jax
import jax.numpy as jnp
from jax import lax

D = 768
HEADS = 12
HD = 64
FF = 3072
PATCHES = 577
ROWS_DEV = 8
SLOTS = 289
ROWS = 64
TOKENS = 36928
INNER = 768
N_TOK = 8


def patch_layout(base_key):
    slots_owned = ROWS_DEV * SLOTS
    deficit = slots_owned // 16
    last_short = deficit // ROWS_DEV
    spread_part = deficit - last_short
    live_count = slots_owned - deficit
    item_count = ROWS_DEV * PATCHES
    weights = jax.random.randint(jax.random.fold_in(base_key, 11), (N_TOK, ROWS_DEV), 1, 100)
    weights = weights.at[:, ROWS_DEV - 1].set(0)
    running = jnp.cumsum(weights, axis=1)
    whole_weight = jnp.maximum(running[:, -1:], 1)
    cut_points = spread_part * running // whole_weight
    cut_points = cut_points.at[:, ROWS_DEV - 1].set(deficit)
    shortfall = cut_points - jnp.concatenate([jnp.zeros((N_TOK, 1), jnp.int32), cut_points[:, :-1]], axis=1)
    counts = SLOTS - shortfall
    starts = jnp.cumsum(counts, axis=1) - counts
    serial = jnp.arange(item_count, dtype=jnp.int32)
    picked = serial < live_count
    live_serial = jnp.where(picked, serial, 0)
    buffer_of = jnp.sum((live_serial[None, :, None] >= starts[:, None, :]).astype(jnp.int32), axis=2) - 1
    begin_slot = jnp.take_along_axis(starts, buffer_of, axis=1)
    within = live_serial[None, :] - begin_slot
    owners = jnp.arange(N_TOK, dtype=jnp.int32)[:, None]
    slot_item = jnp.where(picked[None, :], owners * slots_owned + buffer_of * SLOTS + within, -1)
    image_cuts = jax.random.randint(jax.random.fold_in(base_key, 12), (N_TOK, ROWS_DEV, 3), 1, SLOTS)
    item_cuts = jnp.take_along_axis(image_cuts, jnp.broadcast_to(buffer_of[:, :, None], (N_TOK, item_count, 3)), axis=1)
    image_live = jnp.sum((item_cuts <= within[:, :, None]).astype(jnp.int32), axis=2)
    image_rest = jax.random.randint(jax.random.fold_in(base_key, 13), (N_TOK, item_count), 0, 4)
    image_item = jnp.where(picked[None, :], image_live, image_rest)
    order_serial = jnp.where(picked, serial, serial - live_count)
    source = (owners + order_serial[None, :]) % N_TOK
    shuffle = jax.random.permutation(jax.random.fold_in(base_key, 14), N_TOK * item_count).reshape(N_TOK, item_count)
    sort_key = (source * (N_TOK * item_count) + shuffle).reshape(-1)
    arrangement = jnp.argsort(sort_key, stable=True)
    return (slot_item.reshape(-1)[arrangement], image_item.reshape(-1)[arrangement])


def draw_slot_index(key, part):
    return patch_layout(key)[0].astype(jnp.int32)


def draw_segment(key, part):
    return patch_layout(key)[1].astype(jnp.int32)


def norm_pair(base_key):
    gain_key, shift_key = jax.random.split(base_key)
    gain_row = jnp.clip(1.0 + 0.15 * jax.random.normal(gain_key, (D,), jnp.float32), 0.7, 1.3)
    shift_row = jnp.clip(0.3 * jax.random.normal(shift_key, (D,), jnp.float32), -0.6, 0.6)
    return jnp.stack([gain_row, shift_row]).astype(jnp.float32)


def draw_first_norm(key, part):
    return norm_pair(jax.random.fold_in(key, 21))


def draw_second_norm(key, part):
    return norm_pair(jax.random.fold_in(key, 22))


def block_levels(stream_key, shape, shards, smallest, high):
    level, own = 1.0, jax.random.fold_in(stream_key, 6)
    for dim, blocks in shards:
        heights = jnp.exp(jax.random.uniform(jax.random.fold_in(own, dim), (blocks,), jnp.float32, smallest / len(shards), high / len(shards)))
        level = level * jnp.repeat(heights, shape[dim] // blocks).reshape([-1 if axis == dim else 1 for axis in range(len(shape))])
    return level


def centred(rng, shape, scale, reach, cuts=(), held_as=jnp.bfloat16):
    factor_of = block_levels(rng, shape, cuts, -0.22, 0.18) if cuts else 1.0
    array = jax.random.normal(rng, shape, jnp.float32) * scale * factor_of
    return jnp.minimum(jnp.maximum(array, -reach), reach).astype(held_as)


def setup_inputs(seed: int = 0) -> dict:
    seeds = jax.random.split(jax.random.key(seed), 16)
    return {
        "tokens": centred(seeds[0], (TOKENS, D), 1.0, 6.0, ((0, 8),)),
        "slot_index": draw_slot_index(jax.random.fold_in(seeds[15], 71), 0),
        "segment": draw_segment(jax.random.fold_in(seeds[15], 71), 0),
        "router": centred(seeds[3], (D,), D ** -0.5, 0.21875, (), jnp.float32),
        "first_norm": draw_first_norm(jax.random.fold_in(seeds[15], 71), 0),
        "qkv_weight": centred(seeds[5], (D, 3, INNER), D ** -0.5, 0.21875, ((2, 4),)),
        "qv_bias": centred(seeds[6], (2, INNER), 0.3, 4.0, ((1, 4),), jnp.float32),
        "out_weight": centred(seeds[7], (INNER, D), (INNER // 64) ** -0.5, 1.75, ((0, 4),)),
        "out_bias": centred(seeds[8], (D,), 0.3, 4.0, ((0, 4),), jnp.float32),
        "second_norm": draw_second_norm(jax.random.fold_in(seeds[15], 71), 0),
        "up_weight": centred(seeds[10], (D, FF), D ** -0.5, 0.21875, ((1, 4),)),
        "up_bias": centred(seeds[11], (FF,), 0.3, 4.0, ((0, 4),), jnp.float32),
        "down_weight": centred(seeds[12], (FF, D), FF ** -0.5, 0.109375, ((0, 4),)),
        "down_bias": centred(seeds[13], (D,), 0.3, 4.0, ((0, 4),), jnp.float32),
        "cotangent": centred(seeds[14], (TOKENS, D), 1.0, 6.0, ((0, 8),)),
    }


HIGHEST_PRECISION = lax.Precision.HIGHEST
EPSILON = 1e-06
MASKED_SCORE = -1000000000.0

@jax.custom_vjp
def low(v):
    return lax.optimization_barrier(v.astype(jnp.bfloat16)).astype(jnp.float32)

@jax.custom_vjp
def low_back(v):
    return v

def low_keep(v):
    return (low(v), None)

def low_pass(kept, grad):
    return (grad,)

def back_keep(v):
    return (v, None)

def back_low(kept, grad):
    return (low(grad),)
low.defvjp(low_keep, low_pass)
low_back.defvjp(back_keep, back_low)

def normalize(values, gain_row, shift_row):
    row_mean = lax.optimization_barrier(jnp.mean(values, axis=-1, keepdims=True))
    centered = values - row_mean
    variance = lax.optimization_barrier(jnp.mean(centered * centered, axis=-1, keepdims=True))
    return centered * lax.rsqrt(variance + EPSILON) * gain_row + shift_row

def attend_rows(query_rows, key_rows, value_rows, allowed):
    scores = low_back(HD ** (-0.5) * jnp.einsum('rqhe,rkhe->rhqk', query_rows, key_rows, precision=HIGHEST_PRECISION))
    scores = jnp.where(allowed[:, None], scores, MASKED_SCORE)
    weights = low(jax.nn.softmax(scores, axis=-1))
    return jnp.einsum('rhqk,rkhe->rqhe', weights, value_rows, precision=HIGHEST_PRECISION)

def attend_group(group):
    return jax.checkpoint(attend_rows)(group[0], group[1], group[2], group[3])

def reference(tokens, slot_index, segment, router, first_norm, qkv_weight, qv_bias, out_weight, out_bias, second_norm, up_weight, up_bias, down_weight, down_bias, cotangent):
    slot_total = ROWS * SLOTS
    chosen = slot_index >= 0
    target = jnp.where(chosen, slot_index, slot_total).astype(jnp.int32)
    fetch_index = jnp.minimum(target, slot_total - 1).astype(jnp.int32)
    chosen_float = chosen.astype(jnp.float32)
    slot_segment = jnp.full((slot_total,), -1, jnp.int32).at[target].set(segment.astype(jnp.int32), mode='drop')
    slot_segment = slot_segment.reshape(N_TOK, ROWS_DEV, SLOTS)
    allowed = (slot_segment[:, :, :, None] == slot_segment[:, :, None, :]) & (slot_segment[:, :, None, :] >= 0)
    group_shape = (N_TOK, ROWS_DEV, SLOTS, HEADS, HD)

    def forward(inputs, router_row, norm_one, qkv_full, bias_pair, out_full, out_shift, norm_two, up_full, up_shift, down_full, down_shift):
        normed = low_back(low(normalize(inputs, norm_one[0], norm_one[1])))
        buffers = jnp.zeros((slot_total, D), jnp.float32).at[target].set(normed, mode='drop')
        query_all = low_back(low(jnp.dot(buffers, qkv_full[:, 0], precision=HIGHEST_PRECISION) + bias_pair[0]))
        key_all = low_back(low(jnp.dot(buffers, qkv_full[:, 1], precision=HIGHEST_PRECISION)))
        value_all = low_back(low(jnp.dot(buffers, qkv_full[:, 2], precision=HIGHEST_PRECISION) + bias_pair[1]))
        attended = lax.map(attend_group, (query_all.reshape(group_shape), key_all.reshape(group_shape), value_all.reshape(group_shape), allowed))
        heads_all = low_back(low(attended.reshape(slot_total, INNER)))
        returned = low_back(low(jnp.dot(heads_all, out_full, precision=HIGHEST_PRECISION) + out_shift))
        gate_value = jax.nn.sigmoid(jnp.dot(inputs, router_row, precision=HIGHEST_PRECISION))
        residual = inputs + (chosen_float * gate_value)[:, None] * returned[fetch_index]
        second = low(normalize(residual, norm_two[0], norm_two[1]))
        pre_hidden = low_back(jnp.dot(second, up_full, precision=HIGHEST_PRECISION) + up_shift)
        hidden = low(jax.nn.gelu(pre_hidden, approximate=False))
        return residual + jnp.dot(hidden, down_full, precision=HIGHEST_PRECISION) + down_shift
    floats = (tokens.astype(jnp.float32), router, first_norm, qkv_weight.astype(jnp.float32), qv_bias, out_weight.astype(jnp.float32), out_bias, second_norm, up_weight.astype(jnp.float32), up_bias, down_weight.astype(jnp.float32), down_bias)
    result, pullback = jax.vjp(forward, *floats)
    gradients = pullback(cotangent.astype(jnp.float32))
    return (result.astype(jnp.bfloat16), gradients[0], gradients[3], gradients[4], gradients[5], gradients[6], gradients[8], gradients[9], gradients[10], gradients[11], gradients[2], gradients[7], gradients[1])
```

```python
import jax
import jax.numpy as jnp
from jax import lax
from jax.sharding import PartitionSpec as P

HD = 64
ROWS_DEV = 8
SLOTS = 289
EPSILON = 1e-06
MASKED_SCORE = -1000000000.0
BF = jnp.bfloat16
F32 = jnp.float32
EXACT = lax.Precision.HIGHEST


def ceil_to(value, step):
    return -(-value // step) * step


def normal_parts(values):
    row_mean = jnp.mean(values, axis=-1, keepdims=True)
    centered = values - row_mean
    inverse = lax.rsqrt(jnp.mean(centered * centered, axis=-1, keepdims=True) + EPSILON)
    return centered * inverse, inverse


def norm_back(grad_in, normal, inverse, gain_row):
    scaled = grad_in * gain_row
    return inverse * (
        scaled
        - jnp.mean(scaled, axis=-1, keepdims=True)
        - normal * jnp.mean(scaled * normal, axis=-1, keepdims=True)
    )


def mul(left, right):
    return lax.dot_general(left, right, (((1,), (0,)), ((), ())), preferred_element_type=F32)


def mul_t0(left, right):
    return lax.dot_general(left, right, (((0,), (0,)), ((), ())), preferred_element_type=F32)


def mul_t1(left, right):
    return lax.dot_general(left, right, (((1,), (1,)), ((), ())), preferred_element_type=F32)


def hot(rows, cols):
    return (rows[:, None] == cols[None, :]).astype(BF)


def columns_of(source, part, shares):
    width = source.shape[-1] // shares
    return lax.dynamic_slice_in_dim(source, part * width, width, source.ndim - 1)


def body(
    tokens,
    slot_index,
    segment,
    router,
    first_norm,
    qkv_weight,
    qv_bias,
    out_weight,
    out_bias,
    second_norm,
    up_weight,
    up_bias,
    down_weight,
    down_bias,
    cotangent,
):
    peers = lax.axis_size("tok")
    shares = lax.axis_size("tp")
    part = lax.axis_index("tp")
    half_bit = part % 2
    pair_bit = part // 2
    half_swap = [(i, i ^ 1) for i in range(shares)]
    pair_swap = [(i, i ^ 2) for i in range(shares)]
    count, width = tokens.shape
    inner = qkv_weight.shape[2]
    heads_local = inner // HD
    owned = ROWS_DEV * SLOTS
    live = owned - owned // 16
    capacity = -(-live // peers)
    quarter = -(-capacity // shares)
    block = ceil_to(quarter + 1, 8)
    picked = peers * block
    idle_share = -(-(count - live) // shares)
    idle = ceil_to(idle_share, 16)
    own = picked + idle

    chosen = slot_index >= 0
    owner = jnp.where(chosen, slot_index // owned, peers)
    lanes = jnp.arange(peers, dtype=jnp.int32)
    match = (owner[:, None] == lanes[None, :]).astype(jnp.int32)
    rank = jnp.sum(jnp.cumsum(match, axis=0) * match, axis=1) - 1
    idle_rank = jnp.cumsum(jnp.where(chosen, 0, 1)) - 1
    piece = rank // quarter
    offset = rank % quarter
    mine = chosen & (piece % 2 == half_bit)
    far = (piece // 2) ^ pair_bit
    send_row = jnp.where(mine, (owner * 2 + far) * block + offset, -1)
    picked_row = jnp.where(mine & (far == 0), owner * block + offset, -1)
    own_row = jnp.where(
        chosen,
        picked_row,
        jnp.where(idle_rank // idle_share == part, picked + idle_rank % idle_share, -1),
    )
    back_picked = jnp.where(chosen, piece * picked + owner * block + offset, -1)
    back_idle = jnp.where(chosen, -1, (idle_rank // idle_share) * idle + idle_rank % idle_share)

    up_all = lax.all_gather(up_weight, "tp")
    down_all = lax.all_gather(down_weight, "tp")

    send_hot = hot(jnp.arange(2 * picked, dtype=jnp.int32), send_row)
    own_hot = hot(jnp.arange(own, dtype=jnp.int32), own_row)
    send_in = mul(send_hot, tokens)
    send_hat, _ = normal_parts(send_in)
    send_rows = (send_hat * first_norm[0] + first_norm[1]).astype(BF)
    local_slot = jnp.where(chosen, slot_index % owned, 0)
    marks = jnp.stack([local_slot // 64 + 1, local_slot % 64, segment])
    block_of = jnp.where(mine, owner * 2 + far, -1)
    block_hot = (jnp.arange(2 * peers, dtype=jnp.int32)[:, None] == block_of[None, :])
    mark_left = jnp.where(block_hot[None], marks[:, None, :], 0).astype(BF)
    mark_right = hot(offset, jnp.arange(128, dtype=jnp.int32))
    mark_rows = mul(mark_left.reshape(6 * peers, count), mark_right).astype(BF)
    mark_rows = mark_rows.reshape(3, 2 * peers, 128).transpose(1, 0, 2).reshape(2 * peers, 1, 384)
    mark_rows = jnp.pad(mark_rows, ((0, 0), (0, 0), (0, width - 384)))
    row_kind = jnp.arange(block, dtype=jnp.int32)[None, :, None] == quarter
    send_rows = jnp.where(row_kind, mark_rows, send_rows.reshape(2 * peers, block, width))
    got_near = lax.all_to_all(
        send_rows.reshape(peers, 2, block, width), "tok", split_axis=0, concat_axis=0, tiled=True
    )
    got_far = lax.ppermute(got_near, "tp", half_swap)
    got = jnp.stack([got_near, got_far])
    mark = got[:, :, :, quarter, :].astype(jnp.int32)
    recv_slot = (mark[..., 0:block] - 1) * 64 + mark[..., 128 : 128 + block]
    recv_segment = mark[..., 256 : 256 + block]
    slot_rows = recv_slot.transpose(0, 2, 1, 3).reshape(4 * picked)
    segment_rows = recv_segment.transpose(0, 2, 1, 3).reshape(4 * picked)
    features = got.transpose(0, 2, 1, 3, 4).reshape(4 * picked, width)

    pad = 304
    ids = jnp.arange(ROWS_DEV * pad, dtype=jnp.int32)
    slot_ids = jnp.where(ids % pad < SLOTS, (ids // pad) * SLOTS + ids % pad, -1000)
    slot_hot = hot(slot_ids, slot_rows)
    slot_features = mul(slot_hot, features).astype(BF)
    flat_weight = qkv_weight.reshape(width, 3 * inner)
    bias_row = jnp.concatenate([qv_bias[0], jnp.zeros_like(qv_bias[0]), qv_bias[1]])
    slot_qkv = (mul(slot_features, flat_weight) + bias_row).astype(BF)
    slot_segment = (
        jnp.sum(jnp.where(slot_hot > 0, segment_rows[None, :] + 1, 0), axis=1) - 1
    ).reshape(ROWS_DEV, pad)
    allowed = (slot_segment[:, :, None] == slot_segment[:, None, :]) & (
        slot_segment[:, None, :] >= 0
    )
    grouped = slot_qkv.reshape(ROWS_DEV, pad, 3, heads_local, HD)
    query, key, value = grouped[:, :, 0], grouped[:, :, 1], grouped[:, :, 2]
    score_scale = HD ** (-0.5)
    scores = (
        jnp.einsum("rqhe,rkhe->rhqk", query, key, preferred_element_type=F32) * score_scale
    )
    scores = jnp.where(allowed[:, None], scores, MASKED_SCORE)
    top = jnp.max(scores, axis=-1, keepdims=True)
    raised = jnp.exp(scores - top)
    weights = raised / jnp.sum(raised, axis=-1, keepdims=True)
    weights_low = weights.astype(BF)
    attended = jnp.einsum("rhqk,rkhe->rqhe", weights_low, value, preferred_element_type=F32)
    heads = attended.reshape(ROWS_DEV * pad, inner).astype(BF)
    heads_rows = mul_t0(slot_hot, heads).astype(BF)
    bias_full = lax.dynamic_update_slice(
        jnp.zeros((width,), F32), out_bias, (part * (width // shares),)
    )

    def share_sum(partial):
        near, far_half = partial[: 2 * picked], partial[2 * picked :]
        got_half = lax.ppermute(far_half.astype(BF), "tp", half_swap)
        joined = near + got_half.astype(F32)
        got_pair = lax.ppermute(joined[picked:].astype(BF), "tp", pair_swap)
        return (joined[:picked] + got_pair.astype(F32)).astype(BF)

    def across(rows):
        return lax.all_to_all(
            rows.reshape(peers, block, width), "tok", split_axis=0, concat_axis=0, tiled=True
        ).reshape(picked, width)

    returned = across(share_sum(mul(heads_rows, out_weight) + bias_full))

    own_in = mul(own_hot, tokens)
    own_cot_low = mul(own_hot, cotangent).astype(BF)
    own_cot = own_cot_low.astype(F32)
    gate = jax.nn.sigmoid(jnp.dot(own_in, router, precision=EXACT))
    branch = jnp.pad(returned.astype(F32), ((0, idle), (0, 0)))
    scale = jnp.where(jnp.arange(own) < picked, gate, 0.0)
    residual = own_in + scale[:, None] * branch
    second_hat, second_inv = normal_parts(residual)
    second = (second_hat * second_norm[0] + second_norm[1]).astype(BF)
    up_cols = up_all.transpose(1, 0, 2).reshape(width, -1)
    down_rows = down_all.reshape(-1, width)
    up_bias_all = lax.all_gather(up_bias, "tp", tiled=True)
    down_bias_all = lax.all_gather(down_bias, "tp", tiled=True)
    pre = mul(second, up_cols) + up_bias_all
    below = 0.5 * (1.0 + lax.erf(pre * (2.0**-0.5)))
    bell = jnp.exp(-0.5 * pre * pre) * (2.0 * jnp.pi) ** -0.5
    hidden = (pre * below).astype(BF)
    layer_rows = (residual + mul(hidden, down_rows) + down_bias_all).astype(BF)
    d_hidden = mul_t1(own_cot_low, down_rows)
    d_pre = (d_hidden * (below + pre * bell)).astype(BF)
    d_down = mul_t0(hidden, own_cot_low).astype(BF).reshape(shares, -1, width)
    d_up = mul_t0(second, d_pre).astype(BF)
    d_up = d_up.reshape(width, shares, -1).transpose(1, 0, 2)
    d_second = mul_t1(d_pre, up_cols)
    d_residual = own_cot + norm_back(d_second, second_hat, second_inv, second_norm[0])
    d_branch = (d_residual[:picked] * scale[:picked, None]).astype(BF)
    d_logit = jnp.sum(d_residual * branch, axis=1) * scale * (1.0 - gate)
    small = jnp.concatenate(
        [
            jnp.sum(d_pre.astype(F32), axis=0).reshape(shares, width),
            jnp.stack(
                [
                    jnp.sum(d_second * second_hat, axis=0),
                    jnp.sum(d_second, axis=0),
                    jnp.sum(own_cot, axis=0),
                    jnp.sum(d_branch.astype(F32), axis=0),
                    jnp.sum(d_logit[:, None] * own_in, axis=0),
                ]
            ),
        ]
    )
    d_up_share = lax.psum_scatter(d_up, "tp", scatter_dimension=0)
    d_down_share = lax.psum_scatter(d_down, "tp", scatter_dimension=0)
    d_up_total = lax.psum(d_up_share, "tok").astype(F32)
    d_down_total = lax.psum(d_down_share, "tok").astype(F32)

    grad_own = across(d_branch)
    grad_near = jnp.concatenate([grad_own, lax.ppermute(grad_own, "tp", pair_swap)])
    grad_rows = jnp.concatenate([grad_near, lax.ppermute(grad_near, "tp", half_swap)])
    d_out_weight = mul_t0(heads_rows, grad_rows)
    d_heads_rows = mul_t1(grad_rows, out_weight).astype(BF)
    d_heads = mul(slot_hot, d_heads_rows).astype(BF).reshape(ROWS_DEV, pad, heads_local, HD)
    d_weights = jnp.einsum("rqhe,rkhe->rhqk", d_heads, value, preferred_element_type=F32)
    d_value = jnp.einsum("rhqk,rqhe->rkhe", weights_low, d_heads, preferred_element_type=F32)
    d_scores = (
        weights * (d_weights - jnp.sum(weights * d_weights, axis=-1, keepdims=True))
    ).astype(BF)
    d_query = (
        jnp.einsum("rhqk,rkhe->rqhe", d_scores, key, preferred_element_type=F32) * score_scale
    )
    d_key = (
        jnp.einsum("rhqk,rqhe->rkhe", d_scores, query, preferred_element_type=F32) * score_scale
    )
    d_qkv = (
        jnp.stack([d_query, d_key, d_value], axis=2).astype(BF).reshape(ROWS_DEV * pad, 3 * inner)
    )
    d_qkv_weight = mul_t0(slot_features, d_qkv)
    d_qkv_bias = jnp.sum(d_qkv.astype(F32), axis=0).reshape(3, inner)
    d_qv_bias = jnp.stack([d_qkv_bias[0], d_qkv_bias[2]])
    d_qkv_rows = mul_t0(slot_hot, d_qkv).astype(BF)
    d_normed = across(share_sum(mul_t1(d_qkv_rows, flat_weight))).astype(F32)
    d_qkv_total = lax.psum(d_qkv_weight.astype(BF), "tok").astype(F32)
    d_out_total = lax.psum(d_out_weight.astype(BF), "tok").astype(F32)

    first_hat, first_inv = normal_parts(own_in[:picked])
    d_picked = (
        d_residual[:picked]
        + norm_back(d_normed, first_hat, first_inv, first_norm[0])
        + d_logit[:picked, None] * router[None, :]
    ).astype(BF)
    d_idle = d_residual[picked:].astype(BF)

    def to_columns(rows):
        pieces = rows.reshape(rows.shape[0], shares, width // shares).transpose(1, 0, 2)
        return lax.all_to_all(pieces, "tp", split_axis=0, concat_axis=0, tiled=True).reshape(
            shares * rows.shape[0], width // shares
        )

    picked_hot = hot(back_picked, jnp.arange(shares * picked, dtype=jnp.int32))
    idle_hot = hot(back_idle, jnp.arange(shares * idle, dtype=jnp.int32))
    layer_out = (
        mul(picked_hot, to_columns(layer_rows[:picked]))
        + mul(idle_hot, to_columns(layer_rows[picked:]))
    ).astype(BF)
    d_tokens = mul(picked_hot, to_columns(d_picked)) + mul(idle_hot, to_columns(d_idle))
    first_pair = jnp.stack([jnp.sum(d_normed * first_hat, axis=0), jnp.sum(d_normed, axis=0)])
    small = lax.psum(jnp.concatenate([small, first_pair]), ("tok", "tp"))
    small_cols = columns_of(small[shares:], part, shares)
    d_up_bias = lax.dynamic_slice_in_dim(small, part, 1, 0).reshape(width)
    d_qv_bias = lax.psum(d_qv_bias, "tok")
    return (
        layer_out,
        d_tokens,
        d_qkv_total.reshape(width, 3, inner),
        d_qv_bias,
        d_out_total,
        small_cols[3],
        d_up_total,
        d_up_bias,
        d_down_total,
        small_cols[2],
        small_cols[5:7],
        small_cols[0:2],
        small_cols[4],
    )


def solution(mesh):
    return jax.shard_map(
        body,
        mesh=mesh,
        in_specs=(
            P("tok", None),
            P("tok"),
            P("tok"),
            P(),
            P(),
            P(None, None, "tp"),
            P(None, "tp"),
            P("tp", None),
            P("tp"),
            P(),
            P(None, "tp"),
            P("tp"),
            P("tp", None),
            P("tp"),
            P("tok", None),
        ),
        out_specs=(
            P("tok", "tp"),
            P("tok", "tp"),
            P(None, None, "tp"),
            P(None, "tp"),
            P("tp", None),
            P("tp"),
            P(None, "tp"),
            P("tp"),
            P("tp", None),
            P("tp"),
            P(None, "tp"),
            P(None, "tp"),
            P("tp"),
        ),
        check_vma=False,
    )
```
